32 devices in a mesh: dp: 4 (over x, core), ctx: 8 (over z, y).
Axes of the slice: x: 2, y: 2, z: 4, core: 2. Of those that a mesh axis runs over, the one named last changes fastest.
Arguments:
- merged_grad: bfloat16 [4096, 1792], P(('dp', 'ctx')), may hold values from -6 to 6
- merged_owner: int32 [4096, 1], P(('dp', 'ctx')), may hold values from 0 to 7; in each aligned block of 128 rows (0 to 127, 128 to 255, ...) at most 32 rows name the same one
- merger_pre: bfloat16 [8192, 2560], P(('dp', 'ctx')), may hold values from -6 to 6
- fc2_weight: bfloat16 [2560, 1792], P('ctx'), may hold values from -0.125 to 0.125
- query: bfloat16 [8192, 1280], P(('dp', 'ctx')), may hold values from -32 to 32
- key_states: bfloat16 [8192, 1280], P(('dp', 'ctx')), may hold values from -32 to 32
- value_states: bfloat16 [8192, 1280], P(('dp', 'ctx')), may hold values from -6 to 6
- out_grad: bfloat16 [8192, 1280], P(('dp', 'ctx')), may hold values from -6 to 6
- position: int32 [2, 8192], P(None, ('dp', 'ctx')), may hold values from 0 to 63, as said below
Outputs:
- hidden_grad: bfloat16 [8192, 2560], P(('dp', 'ctx'))
- weight_grad: float32 [2560, 1792], P('ctx', 'dp')
- query_grad: bfloat16 [8192, 1280], P(('dp', 'ctx'))
- key_grad: bfloat16 [8192, 1280], P(('dp', 'ctx'))
- value_grad: bfloat16 [8192, 1280], P(('dp', 'ctx'))
The draws below stay inside these ranges and needn't reach their ends.
Inputs may be any that keep to these rules, and one draw needn't show every extreme that they name: `merged_owner`: in each device's block of 128 rows no owner is named more than 32 times. `position`: each window of 64 consecutive patches covers an aligned square of 8 by 8 grid positions, row by row.
All inputs are finite; a program needn't handle non-finite values.
Results may differ from the reference program's by a relative error of at most 0.0017.
The reference program's roundings to bfloat16 on the way (of `slotted`, `act`, `q_rot`, `k_rot`, `probs_b` and `score_grad`) count: a program that leaves them out, or rounds other values in their place, can miss the bound.
Values may be sent and summed in bfloat16 or wider, within the bound.
A program may use at most 128 MiB of HBM per device.

```python
import math
import jax
import jax.numpy as jnp
import numpy as np
from jax import lax

D = 1280
HEADS = 16
HEAD = 80
WIN_SIDE = 8
WIN = 64
HID = 2560
OUTW = 1792
G_DEV = 128
PATCH_DEV = 256
CAP = 32
SLOTS = 256
TOKENS = 4096
ALLSLOTS = 8192
PATCHES = 8192
N_DP = 4
N_CTX = 8


def window_positions(key):
    pkey = jax.random.fold_in(key, 7)
    windows = PATCHES // WIN
    corner = jax.random.randint(pkey, (2, windows), 0, WIN_SIDE, dtype=jnp.int32)
    inside = jnp.arange(WIN, dtype=jnp.int32)
    rows = corner[0][:, None] * WIN_SIDE + inside[None, :] // WIN_SIDE
    cols = corner[1][:, None] * WIN_SIDE + inside[None, :] % WIN_SIDE
    return jnp.stack([rows.reshape(-1), cols.reshape(-1)])


def drawn_pair(key):
    query = jax.random.normal(jax.random.fold_in(key, 11), (PATCHES, HEADS, HEAD), jnp.float32)
    keys = jax.random.normal(jax.random.fold_in(key, 12), (PATCHES, HEADS, HEAD), jnp.float32)
    return (query.reshape(PATCHES, D), keys.reshape(PATCHES, D))


def draw_query(key, part):
    return drawn_pair(key)[0].astype(jnp.bfloat16)


def draw_key_states(key, part):
    return drawn_pair(key)[1].astype(jnp.bfloat16)


def draw_position(key, part):
    return window_positions(key)


def with_spikes(entries, rng, source, target, parts, factor):
    def block_of(dim):
        return (jnp.arange(entries.shape[dim]) // (entries.shape[dim] // parts)).reshape((-1,) + (1,) * (entries.ndim - 1 - dim))

    first = jax.random.permutation(rng, parts)[block_of(target)]
    far = (block_of(target) + parts // 2) % parts
    return jnp.where((block_of(source) == first) | (block_of(source) == far), factor * entries, entries)


def block_scale(key, dims, split, low, top_value):
    gain, own = 1.0, jax.random.fold_in(key, 6)
    for dim, blocks in split:
        steps = jnp.exp(jax.random.uniform(jax.random.fold_in(own, dim), (blocks,), jnp.float32, low / len(split), top_value / len(split)))
        gain = gain * jnp.repeat(steps, dims[dim] // blocks).reshape([-1 if axis == dim else 1 for axis in range(len(dims))])
    return gain


def routed_block(key, own, number, rows, amount, top, reach, lean):
    sequence = jax.random.permutation(key, amount)
    heavy_load, usual = load_shares(amount, rows * top, reach, lean, True), load_shares(amount, rows * top, reach, lean, False)
    places = jnp.arange(amount)

    def named(tallies, turn):
        used = int((tallies > 0).sum())
        fixed = max(1, used // 4)
        moved = fixed + (places - fixed + turn * (used - fixed)) % max(1, amount - fixed)
        return jnp.zeros((amount,), jnp.int32).at[sequence[jnp.where(places < fixed, places, moved)]].set(jnp.asarray(tallies, jnp.int32))

    tallies = jnp.where(number % 4 == 0, named(heavy_load, number // 4), named(usual, number - number // 4 - 1))
    mixed = jax.random.permutation(jax.random.fold_in(own, 3), amount)
    source_of, sink = mixed[0:amount // 2 * 2:2], mixed[1:amount // 2 * 2:2]
    slack = jnp.minimum(tallies[source_of] - 1, reach - tallies[sink]) // 2
    slack = jnp.where((source_of == sequence[0]) | (sink == sequence[0]) | (tallies[sink] == 0), 0, jnp.maximum(slack, 0))
    moved = jax.random.randint(jax.random.fold_in(own, 4), (amount // 2,), 0, 1 << 20) % (slack + 1)
    tallies = tallies.at[source_of].add(-moved).at[sink].add(moved)
    members = jnp.searchsorted(jnp.cumsum(tallies), jnp.arange(rows * top), side="right").astype(jnp.int32)
    grid = members.reshape(top, rows).T
    grid = grid[jax.random.permutation(jax.random.fold_in(own, 1), rows)]
    turn = jax.random.randint(jax.random.fold_in(own, 2), (rows, 1), 0, top)
    return jnp.take_along_axis(grid, (jnp.arange(top)[None, :] + turn) % top, axis=1)


def load_shares(count, total, bound, skew, full):
    weights = [(1 << 20) // math.isqrt(standing ** skew) + 1 for standing in range(1, count + 1)]
    largest = bound if full else min(bound, max(-(-total // count), total * weights[0] // sum(weights)))
    least = 1 if total - largest >= count - 1 else 0
    given, spare = [largest] + [least] * (count - 1), total - largest - least * (count - 1)
    while spare > 0:
        movable = [i for i in range(1, count) if given[i] < largest] or [i for i in range(1, count) if given[i] < bound]
        pool, left = sum([weights[i] for i in movable]), spare
        for i in movable:
            extra = min(bound - given[i], max(1, left * weights[i] // pool), spare)
            given[i] = given[i] + extra
            spare = spare - extra
    return np.array(given)


def noise(stream_key, dims, deviation, limit, cuts=(), held_as=jnp.bfloat16):
    values = deviation * jax.random.normal(stream_key, dims, jnp.float32)
    if cuts:
        values = values * block_scale(stream_key, dims, cuts, -0.22, 0.18)
    return jnp.clip(values, -limit, limit).astype(held_as)


def gaussian_with(key, extent, width, most, shards, heavy, kind=jnp.bfloat16):
    values = width * jax.random.normal(key, extent, jnp.float32)
    if shards:
        values = values * block_scale(key, extent, shards, -0.22, 0.18)
    return jnp.clip(with_spikes(values, jax.random.fold_in(key, 3), *heavy), -most, most).astype(kind)


def setup_inputs(seed: int = 0) -> dict:
    splits = jax.random.split(jax.random.key(seed), 10)
    merged_grad = noise(splits[0], (TOKENS, OUTW), 1.0, 6.0, ((0, 32),))
    merged_owner_keys = jax.random.split(jax.random.fold_in(splits[1], 1), TOKENS // G_DEV)
    merged_owner_turns = jax.random.permutation(jax.random.fold_in(splits[1], 3), TOKENS // G_DEV)
    merged_owner = jax.vmap(lambda own, number: routed_block(jax.random.fold_in(splits[1], 2), own, number, G_DEV, N_CTX, 1, CAP, 2))(merged_owner_keys, merged_owner_turns).reshape((TOKENS, 1))
    merger_pre = gaussian_with(splits[2], (ALLSLOTS, HID), 1.0, 6.0, ((0, 32),), (0, 1, 32, 2.75))
    fc2_weight = noise(splits[3], (HID, OUTW), HID ** -0.5, 0.125, ((0, 8),))
    query = draw_query(jax.random.fold_in(splits[9], 71), 0)
    key_states = draw_key_states(jax.random.fold_in(splits[9], 71), 0)
    value_states = noise(splits[6], (PATCHES, D), 1.0, 6.0, ((0, 32),))
    out_grad = noise(splits[7], (PATCHES, D), 1.0, 6.0, ((0, 32),))
    position = draw_position(jax.random.fold_in(splits[9], 71), 0)
    return {"merged_grad": merged_grad, "merged_owner": merged_owner, "merger_pre": merger_pre, "fc2_weight": fc2_weight, "query": query, "key_states": key_states, "value_states": value_states, "out_grad": out_grad, "position": position}


def rope_angles(position, head_size):
    quarter = head_size // 4
    freq = 1.0 / (10000.0 ** (jnp.arange(quarter, dtype=jnp.float32) * (4.0 / head_size)))
    rows = position[0].astype(jnp.float32)[:, None] * freq[None, :]
    cols = position[1].astype(jnp.float32)[:, None] * freq[None, :]
    return jnp.concatenate([rows, cols], axis=1)


def rotate(values, angles, sign):
    half = values.shape[-1] // 2
    cosine = jnp.cos(angles)[:, None, :]
    sine = sign * jnp.sin(angles)[:, None, :]
    first = values[..., :half]
    second = values[..., half:]
    return jnp.concatenate([first * cosine - second * sine, second * cosine + first * sine], axis=-1)


def attention_block(query, key_states, value_states, out_grad, position):
    count = query.shape[0]
    windows = count // WIN
    angles = rope_angles(position, HEAD)
    shaped = (count, HEADS, HEAD)
    grouped = (windows, WIN, HEADS, HEAD)
    q_rot = rotate(query.astype(jnp.float32).reshape(shaped), angles, 1.0).astype(jnp.bfloat16)
    k_rot = rotate(key_states.astype(jnp.float32).reshape(shaped), angles, 1.0).astype(jnp.bfloat16)
    q_full = lax.optimization_barrier(q_rot).reshape(grouped).astype(jnp.float32)
    k_full = lax.optimization_barrier(k_rot).reshape(grouped).astype(jnp.float32)
    v_full = value_states.reshape(grouped).astype(jnp.float32)
    g_full = out_grad.reshape(grouped).astype(jnp.float32)
    factor = HEAD ** -0.5
    scores = jnp.einsum("wqhd,wkhd->whqk", q_full, k_full) * factor
    probs = jax.nn.softmax(scores, axis=-1)
    probs_b = lax.optimization_barrier(probs.astype(jnp.bfloat16)).astype(jnp.float32)
    output = jnp.einsum("whqk,wkhd->wqhd", probs_b, v_full)
    value_grad = jnp.einsum("whqk,wqhd->wkhd", probs_b, g_full).astype(jnp.bfloat16)
    prob_grad = jnp.einsum("wqhd,wkhd->whqk", g_full, v_full)
    delta = jnp.transpose(jnp.sum(g_full * output, axis=-1), (0, 2, 1))[..., None]
    score_grad = (probs * (prob_grad - delta)).astype(jnp.bfloat16)
    score_full = lax.optimization_barrier(score_grad).astype(jnp.float32)
    q_grad = jnp.einsum("whqk,wkhd->wqhd", score_full, k_full) * factor
    k_grad = jnp.einsum("whqk,wqhd->wkhd", score_full, q_full) * factor
    query_grad = rotate(q_grad.reshape(shaped), angles, -1.0).astype(jnp.bfloat16).reshape(count, D)
    key_grad = rotate(k_grad.reshape(shaped), angles, -1.0).astype(jnp.bfloat16).reshape(count, D)
    return query_grad, key_grad, value_grad.reshape(count, D)


def reference(merged_grad, merged_owner, merger_pre, fc2_weight, query, key_states, value_states, out_grad, position):
    group_rows = N_CTX * G_DEV
    owner = merged_owner[:, 0].reshape(N_DP, group_rows)
    owners = jnp.arange(N_CTX, dtype=jnp.int32)
    onehot = (owner[:, :, None] == owners[None, None, :]).astype(jnp.int32)
    running = jnp.cumsum(onehot, axis=1, dtype=jnp.int32)
    slot = jnp.sum(running * onehot, axis=2, dtype=jnp.int32) - 1
    group = jnp.arange(N_DP, dtype=jnp.int32)[:, None]
    target = ((group * N_CTX + owner) * SLOTS + slot).reshape(-1).astype(jnp.int32)
    slotted = jnp.zeros((N_DP * N_CTX * SLOTS, OUTW), jnp.bfloat16).at[target].set(merged_grad)

    def merger_group(carry, items):
        slotted_part, pre_part = items
        pre = pre_part.astype(jnp.float32)
        cdf = 0.5 * (1.0 + lax.erf(pre * (0.5 ** 0.5)))
        act = (pre * cdf).astype(jnp.bfloat16)
        slope = cdf + pre * jnp.exp(-0.5 * pre * pre) * ((2.0 * math.pi) ** -0.5)
        linear = jnp.dot(slotted_part, fc2_weight.T, preferred_element_type=jnp.float32)
        hidden = (linear * slope).astype(jnp.bfloat16)
        carry = carry + jnp.dot(act.T, slotted_part, preferred_element_type=jnp.float32)
        return carry, hidden

    weight_sum, hidden = lax.scan(
        merger_group,
        jnp.zeros((HID, OUTW), jnp.float32),
        (slotted.reshape(N_DP * N_CTX, SLOTS, OUTW), merger_pre.reshape(N_DP * N_CTX, SLOTS, HID)),
    )
    hidden_grad = hidden.reshape(N_DP * N_CTX * SLOTS, HID)
    weight_grad = weight_sum * (TOKENS ** -0.5)

    blocks = PATCHES // PATCH_DEV
    stacked = (
        query.reshape(blocks, PATCH_DEV, D),
        key_states.reshape(blocks, PATCH_DEV, D),
        value_states.reshape(blocks, PATCH_DEV, D),
        out_grad.reshape(blocks, PATCH_DEV, D),
        jnp.transpose(position.reshape(2, blocks, PATCH_DEV), (1, 0, 2)),
    )

    def one_block(items):
        return attention_block(items[0], items[1], items[2], items[3], items[4])

    query_grad, key_grad, value_grad = lax.map(one_block, stacked)
    return (
        hidden_grad,
        weight_grad,
        query_grad.reshape(PATCHES, D),
        key_grad.reshape(PATCHES, D),
        value_grad.reshape(PATCHES, D),
    )
```

```python
import functools
import math

import jax
import jax.numpy as jnp
from jax import lax
from jax.experimental import pallas as pl
from jax.experimental.pallas import tpu as pltpu
from jax.sharding import PartitionSpec as P

HEAD = 80
WIN = 64
LANES = 128
F32 = jnp.float32
BF16 = jnp.bfloat16


def rope_tables(position):
    quarter = HEAD // 4
    freq = 1.0 / 10000.0 ** (jnp.arange(quarter, dtype=F32) * (4.0 / HEAD))
    rows = position[0].astype(F32)[:, None] * freq[None, :]
    cols = position[1].astype(F32)[:, None] * freq[None, :]
    angles = jnp.concatenate([rows, cols], axis=1)
    cosine, sine = jnp.cos(angles), jnp.sin(angles)
    pad = jnp.zeros((angles.shape[0], LANES - HEAD), F32)
    return (
        jnp.concatenate([cosine, cosine, pad], axis=1),
        jnp.concatenate([-sine, sine, pad], axis=1),
    )


def spread(table, width):
    shape = (LANES, width)
    lane = lax.broadcasted_iota(jnp.int32, shape, 1) % HEAD
    pick = (lane == lax.broadcasted_iota(jnp.int32, shape, 0)).astype(F32).astype(BF16)
    high = table.astype(BF16)
    rest = table - high.astype(F32)
    mid = rest.astype(BF16)
    low = (rest - mid.astype(F32)).astype(BF16)
    dot = functools.partial(jnp.dot, preferred_element_type=F32)
    return dot(high, pick) + dot(mid, pick) + dot(low, pick)


def attention_kernel(q_ref, k_ref, v_ref, g_ref, c_ref, s_ref, dq_ref, dk_ref, dv_ref):
    width = q_ref.shape[1]
    heads = width // HEAD
    half = HEAD // 2
    cosine = spread(c_ref[...], width)
    sine = spread(s_ref[...], width)
    lane = lax.broadcasted_iota(jnp.int32, (WIN, width), 1)
    first = lane % HEAD < half

    def swap(x):
        return jnp.where(first, pltpu.roll(x, width - half, 1), pltpu.roll(x, half, 1))

    def rotated(x):
        return (x * cosine + swap(x) * sine).astype(BF16)

    def unrotated(x):
        return (x * cosine - swap(x) * sine).astype(BF16)

    q = rotated(q_ref[...].astype(F32))
    k = rotated(k_ref[...].astype(F32))
    v = v_ref[...]
    g = g_ref[...]
    factor = HEAD ** (-0.5)
    nt = (((1,), (1,)), ((), ()))
    tn = (((0,), (0,)), ((), ()))
    nn = (((1,), (0,)), ((), ()))

    def dot(a, b, dims):
        return lax.dot_general(a, b, dims, preferred_element_type=F32)

    dq, dk, dv = {}, {}, {}

    def add(into, tile, value):
        for i in range(value.shape[1] // LANES):
            part = value[:, i * LANES : (i + 1) * LANES]
            into[tile + i] = into[tile + i] + part if tile + i in into else part

    for head in range(heads):
        tile = head * HEAD // LANES
        end = -(-(head + 1) * HEAD // LANES)
        lo, hi = tile * LANES, end * LANES
        here = lax.broadcasted_iota(jnp.int32, (1, hi - lo), 1) + lo
        mask = ((here >= head * HEAD) & (here < (head + 1) * HEAD)).astype(F32).astype(BF16)
        qm = q[:, lo:hi] * mask
        km = k[:, lo:hi] * mask
        gm = g[:, lo:hi] * mask
        scores = dot(qm, k[:, lo:hi], nt) * factor
        weight = jnp.exp(scores - jnp.max(scores, axis=1, keepdims=True))
        probs = weight * (1.0 / jnp.sum(weight, axis=1, keepdims=True))
        probs_b = probs.astype(BF16)
        prob_grad = dot(gm, v[:, lo:hi], nt)
        delta = jnp.sum(probs_b.astype(F32) * prob_grad, axis=1, keepdims=True)
        score_grad = (probs * (prob_grad - delta)).astype(BF16)
        add(dv, tile, dot(probs_b, gm, tn))
        add(dq, tile, dot(score_grad, km, nn))
        add(dk, tile, dot(score_grad, qm, tn))

    def joined(parts):
        return jnp.concatenate([parts[i] for i in range(width // LANES)], axis=1)

    dq_ref[...] = unrotated(joined(dq) * factor)
    dk_ref[...] = unrotated(joined(dk) * factor)
    dv_ref[...] = joined(dv).astype(BF16)


def attention_block(query, key_states, value_states, out_grad, position):
    count, width = query.shape
    cosine, sine = rope_tables(position)
    row = pl.BlockSpec((WIN, width), lambda i: (i, 0))
    table = pl.BlockSpec((WIN, LANES), lambda i: (i, 0))
    return pl.pallas_call(
        attention_kernel,
        grid=(count // WIN,),
        in_specs=[row] * 4 + [table] * 2,
        out_specs=[row] * 3,
        out_shape=[jax.ShapeDtypeStruct((count, width), BF16)] * 3,
        cost_estimate=pl.CostEstimate(
            flops=20_000_000_000, bytes_accessed=14 * count * width, transcendentals=0
        ),
        name="attention",
    )(query, key_states, value_states, out_grad, cosine, sine)


def shards(
    merged_grad,
    merged_owner,
    merger_pre,
    fc2_weight,
    query,
    key_states,
    value_states,
    out_grad,
    position,
):
    rows_here = merged_grad.shape[0]
    owners_count = lax.axis_size("ctx")
    replicas = lax.axis_size("dp")
    slots, units = merger_pre.shape
    mine = units // owners_count
    rows = rows_here * owners_count
    places = slots * owners_count
    owner = lax.all_gather(merged_owner[:, 0], "ctx", axis=0, tiled=True)
    merged = lax.all_gather(merged_grad, "ctx", axis=0, tiled=True)
    pre_sent = jnp.transpose(merger_pre.reshape(slots, owners_count, mine), (1, 0, 2))
    pre_got = lax.all_to_all(pre_sent, "ctx", split_axis=0, concat_axis=0, tiled=True)
    pre_got = pre_got.reshape(places, mine)

    attention = attention_block(query, key_states, value_states, out_grad, position)

    peers = jnp.arange(owners_count, dtype=jnp.int32)
    onehot = (peers[:, None] == owner[None, :]).astype(jnp.int32)
    running = jnp.cumsum(onehot, axis=1, dtype=jnp.int32)
    slot = jnp.sum(running * onehot, axis=0, dtype=jnp.int32) - 1
    target = owner * slots + slot
    place = jnp.arange(places, dtype=jnp.int32)
    landing = (place[:, None] == target[None, :]).astype(BF16)

    pre = lax.dot_general(
        landing, pre_got, (((0,), (0,)), ((), ())), preferred_element_type=F32
    )
    cdf = 0.5 * (1.0 + lax.erf(pre * 0.5**0.5))
    act = (pre * cdf).astype(BF16)
    slope = cdf + pre * jnp.exp(-0.5 * pre * pre) * (2.0 * math.pi) ** (-0.5)
    linear = lax.dot_general(
        merged, fc2_weight, (((1,), (1,)), ((), ())), preferred_element_type=F32
    )
    hidden = (linear * slope).astype(BF16)
    hidden_sent = jnp.dot(landing, hidden, preferred_element_type=F32).astype(BF16)
    hidden_got = lax.all_to_all(
        hidden_sent.reshape(owners_count, slots, mine),
        "ctx",
        split_axis=0,
        concat_axis=0,
        tiled=True,
    )
    hidden_grad = jnp.transpose(hidden_got, (1, 0, 2)).reshape(slots, units)
    partial = lax.dot_general(
        act, merged, (((0,), (0,)), ((), ())), preferred_element_type=F32
    )
    summed = lax.psum_scatter(partial, "dp", scatter_dimension=1, tiled=True)
    weight_grad = summed * (rows * replicas) ** (-0.5)
    return (hidden_grad, weight_grad, *attention)


def solution(mesh):
    every = P(("dp", "ctx"), None)
    return jax.shard_map(
        shards,
        mesh=mesh,
        in_specs=(every, every, every, P("ctx", None)) + (every,) * 4 + (P(None, ("dp", "ctx")),),
        out_specs=(every, P("ctx", "dp")) + (every,) * 3,
        check_vma=False,
    )
```

```python
import functools
import math

import jax
import jax.numpy as jnp
from jax import lax
from jax.experimental import pallas as pl
from jax.experimental.pallas import tpu as pltpu
from jax.sharding import PartitionSpec as P

HEAD = 80
WIN = 64
LANES = 128
F32 = jnp.float32
BF16 = jnp.bfloat16
MESH = pl.DeviceIdType.MESH


def rope_tables(position):
    quarter = HEAD // 4
    freq = 1.0 / 10000.0 ** (jnp.arange(quarter, dtype=F32) * (4.0 / HEAD))
    rows = position[0].astype(F32)[:, None] * freq[None, :]
    cols = position[1].astype(F32)[:, None] * freq[None, :]
    angles = jnp.concatenate([rows, cols], axis=1)
    cosine, sine = jnp.cos(angles), jnp.sin(angles)
    pad = jnp.zeros((angles.shape[0], LANES - HEAD), F32)
    return (
        jnp.concatenate([cosine, cosine, pad], axis=1),
        jnp.concatenate([-sine, sine, pad], axis=1),
    )


def spread(table, width):
    shape = (LANES, width)
    lane = lax.broadcasted_iota(jnp.int32, shape, 1) % HEAD
    pick = (lane == lax.broadcasted_iota(jnp.int32, shape, 0)).astype(F32).astype(BF16)
    high = table.astype(BF16)
    rest = table - high.astype(F32)
    mid = rest.astype(BF16)
    low = (rest - mid.astype(F32)).astype(BF16)
    dot = functools.partial(jnp.dot, preferred_element_type=F32)
    return dot(high, pick) + dot(mid, pick) + dot(low, pick)


def attention_window(w, q_ref, k_ref, v_ref, g_ref, c_ref, s_ref, dq_ref, dk_ref, dv_ref):
    at = pl.ds(pl.multiple_of(w * WIN, WIN), WIN)
    width = q_ref.shape[1]
    heads = width // HEAD
    half = HEAD // 2
    cosine = spread(c_ref[at, :], width)
    sine = spread(s_ref[at, :], width)
    lane = lax.broadcasted_iota(jnp.int32, (WIN, width), 1)
    first = lane % HEAD < half

    def swap(x):
        return jnp.where(first, pltpu.roll(x, width - half, 1), pltpu.roll(x, half, 1))

    def rotated(x):
        return (x * cosine + swap(x) * sine).astype(BF16)

    def unrotated(x):
        return (x * cosine - swap(x) * sine).astype(BF16)

    q = rotated(q_ref[at, :].astype(F32))
    k = rotated(k_ref[at, :].astype(F32))
    v = v_ref[at, :]
    g = g_ref[at, :]
    factor = HEAD ** (-0.5)
    nt = (((1,), (1,)), ((), ()))
    tn = (((0,), (0,)), ((), ()))
    nn = (((1,), (0,)), ((), ()))

    def dot(a, b, dims):
        return lax.dot_general(a, b, dims, preferred_element_type=F32)

    dq, dk, dv = {}, {}, {}

    def add(into, tile, value):
        for i in range(value.shape[1] // LANES):
            part = value[:, i * LANES : (i + 1) * LANES]
            into[tile + i] = into[tile + i] + part if tile + i in into else part

    for head in range(heads):
        tile = head * HEAD // LANES
        end = -(-(head + 1) * HEAD // LANES)
        lo, hi = tile * LANES, end * LANES
        here = lax.broadcasted_iota(jnp.int32, (1, hi - lo), 1) + lo
        mask = ((here >= head * HEAD) & (here < (head + 1) * HEAD)).astype(F32).astype(BF16)
        qm = q[:, lo:hi] * mask
        km = k[:, lo:hi] * mask
        gm = g[:, lo:hi] * mask
        scores = dot(qm, k[:, lo:hi], nt) * factor
        weight = jnp.exp(scores - jnp.max(scores, axis=1, keepdims=True))
        probs = weight * (1.0 / jnp.sum(weight, axis=1, keepdims=True))
        probs_b = probs.astype(BF16)
        prob_grad = dot(gm, v[:, lo:hi], nt)
        delta = jnp.sum(probs_b.astype(F32) * prob_grad, axis=1, keepdims=True)
        score_grad = (probs * (prob_grad - delta)).astype(BF16)
        add(dv, tile, dot(probs_b, gm, tn))
        add(dq, tile, dot(score_grad, km, nn))
        add(dk, tile, dot(score_grad, qm, tn))

    def joined(parts):
        return jnp.concatenate([parts[i] for i in range(width // LANES)], axis=1)

    dq_ref[at, :] = unrotated(joined(dq) * factor)
    dk_ref[at, :] = unrotated(joined(dk) * factor)
    dv_ref[at, :] = joined(dv).astype(BF16)


def fused_kernel(
    owners_count,
    replicas,
    m_ref,
    o_ref,
    p_ref,
    w_ref,
    q_ref,
    k_ref,
    v_ref,
    g_ref,
    c_ref,
    s_ref,
    h_out,
    wg_out,
    dq_ref,
    dk_ref,
    dv_ref,
    mall,
    owners,
    pre_got,
    code,
    act,
    hid,
    hid_out,
    full,
    part,
    part_got,
    m_recv,
    up_sem,
    down_sem,
    side_sem,
    o_send,
    o_recv,
    p_send,
    p_recv,
    h_send,
    h_recv,
    r_send,
    r_recv,
    local_sem,
):
    n = owners_count
    sides = 2
    line = n // sides
    rows_here = m_ref.shape[0]
    mine, slots = pre_got.shape[1:]
    block = sides * rows_here
    blocks = n // sides
    windows = q_ref.shape[0] // WIN
    me = lax.axis_index("ctx")
    rep = lax.axis_index("dp")
    a, b = me // sides, me % sides

    barrier = pltpu.get_barrier_semaphore()
    for r in range(1, n):
        pl.semaphore_signal(barrier, inc=1, device_id={"dp": rep, "ctx": (me + r) % n}, device_id_type=MESH)
    for r in range(1, replicas):
        pl.semaphore_signal(
            barrier, inc=1, device_id={"dp": (rep + r) % replicas, "ctx": me}, device_id_type=MESH
        )
    pl.semaphore_wait(barrier, n - 1 + replicas - 1)

    def send(src, dst, send_sem, recv_sem, ctx=None, dp=None):
        where = {"dp": rep if dp is None else dp, "ctx": me if ctx is None else ctx}
        return pltpu.make_async_remote_copy(
            src_ref=src,
            dst_ref=dst,
            send_sem=send_sem,
            recv_sem=recv_sem,
            device_id=where,
            device_id_type=MESH,
        )

    def owner_copy(r):
        return send(o_ref, owners.at[me], o_send.at[r - 1], o_recv.at[r - 1], ctx=(me + r) % n)

    def pre_copy(r):
        peer = (me + r) % n
        return send(p_ref.at[peer], pre_got.at[me], p_send.at[r - 1], p_recv.at[r - 1], ctx=peer)

    def hidden_copy(r):
        peer = (me + r) % n
        return send(hid_out.at[peer], h_out.at[me], h_send.at[r - 1], h_recv.at[r - 1], ctx=peer)

    def part_copy(r):
        peer = (rep + r) % replicas
        return send(part.at[peer], part_got.at[r - 1], r_send.at[r - 1], r_recv.at[r - 1], dp=peer)

    def up_copy(t, ref):
        return send(ref, mall.at[(a - t) * sides + b], up_sem.at[t], m_recv.at[(a - t) * sides + b], ctx=me + sides)

    def down_copy(t, ref):
        return send(ref, mall.at[(a + t) * sides + b], down_sem.at[t], m_recv.at[(a + t) * sides + b], ctx=me - sides)

    def side_copy(at, ref):
        return send(ref, mall.at[at * sides + b], side_sem.at[at], m_recv.at[at * sides + b], ctx=a * sides + 1 - b)

    def arrived(src):
        send(mall.at[src], mall.at[src], up_sem.at[0], m_recv.at[src], ctx=a * sides + 1 - b).wait_recv()

    for r in range(1, n):
        owner_copy(r).start()

    @pl.when(a + 1 < line)
    def _():
        up_copy(0, m_ref).start()

    @pl.when(a > 0)
    def _():
        down_copy(0, m_ref).start()

    side_copy(a, m_ref).start()
    for r in range(1, n):
        pre_copy(r).start()
    locals_ = [
        pltpu.make_async_copy(m_ref, mall.at[me], local_sem.at[0]),
        pltpu.make_async_copy(o_ref, owners.at[me], local_sem.at[1]),
        pltpu.make_async_copy(p_ref.at[me], pre_got.at[me], local_sem.at[2]),
    ]
    for copy in locals_:
        copy.start()

    def forward(t):
        @pl.when(a - t >= 0)
        def _():
            ref = mall.at[(a - t) * sides + b]
            arrived((a - t) * sides + b)

            @pl.when(a + 1 < line)
            def _():
                up_copy(t, ref).start()

            side_copy(a - t, ref).start()

        @pl.when(a + t < line)
        def _():
            ref = mall.at[(a + t) * sides + b]
            arrived((a + t) * sides + b)

            @pl.when(a > 0)
            def _():
                down_copy(t, ref).start()

            side_copy(a + t, ref).start()

    def with_window(w, carry):
        attention_window(w, q_ref, k_ref, v_ref, g_ref, c_ref, s_ref, dq_ref, dk_ref, dv_ref)

        @pl.when(w + 1 < line)
        def _():
            forward(w + 1)

        return carry

    lax.fori_loop(0, windows, with_window, 0)

    def only_forward(t, carry):
        forward(t)
        return carry

    if windows + 1 < line:
        lax.fori_loop(windows + 1, line, only_forward, 0)

    for copy in locals_:
        copy.wait()
    for r in range(1, n):
        owner_copy(r).wait()

    padded = -(-n // 16) * 16
    earlier = lax.broadcasted_iota(jnp.int32, (rows_here, rows_here), 0) < lax.broadcasted_iota(
        jnp.int32, (rows_here, rows_here), 1
    )
    earlier = earlier.astype(F32).astype(BF16)
    names = lax.broadcasted_iota(jnp.int32, (padded, rows_here), 0)
    base = jnp.zeros((padded, 1), F32)
    for s in range(n):
        onehot = (names == owners[s, 0:1, :]).astype(F32)
        count = jnp.dot(onehot.astype(BF16), earlier, preferred_element_type=F32) + base
        place = jnp.sum(onehot * (count + names.astype(F32) * float(slots)), axis=0, keepdims=True)
        base = base + jnp.sum(onehot, axis=1, keepdims=True)
        lo = s % sides * rows_here
        code[s // sides, :, lo : lo + rows_here] = jnp.broadcast_to(place, (8, rows_here))

    for r in range(1, n):
        pre_copy(r).wait()
    for src in range(line):
        arrived(src * sides + 1 - b)

    standing = lax.broadcasted_iota(jnp.int32, (slots, block), 0).astype(F32)

    def landing(o, t):
        first = (o * slots).astype(F32)
        return (standing == code[t, 0:1, :] - first).astype(F32).astype(BF16)

    def tokens(t, carry):
        def gather(o, total):
            return total + jnp.dot(pre_got[o], landing(o, t), preferred_element_type=F32)

        pre = lax.fori_loop(0, n, gather, jnp.zeros((mine, block), F32))
        cdf = 0.5 * (1.0 + lax.erf(pre * 0.5**0.5))
        slope = cdf + pre * jnp.exp(-0.5 * pre * pre) * (2.0 * math.pi) ** (-0.5)
        rows = jnp.concatenate([mall[t * sides + i] for i in range(sides)], axis=0)
        linear = lax.dot_general(
            w_ref[...], rows, (((1,), (1,)), ((), ())), preferred_element_type=F32
        )
        act[t] = (pre * cdf).astype(BF16)
        hid[t] = (linear * slope).astype(BF16)
        return carry

    lax.fori_loop(0, blocks, tokens, 0)

    def outgoing(o, carry):
        def gather(t, total):
            return total + lax.dot_general(
                hid[t], landing(o, t), (((1,), (1,)), ((), ())), preferred_element_type=F32
            )

        hid_out[o] = lax.fori_loop(0, blocks, gather, jnp.zeros((mine, slots), F32)).astype(BF16)
        return carry

    lax.fori_loop(0, n, outgoing, 0)
    for r in range(1, n):
        hidden_copy(r).start()
    own = pltpu.make_async_copy(hid_out.at[me], h_out.at[me], local_sem.at[3])
    own.start()

    width = full.shape[1]

    def partial(t, carry):
        rows = jnp.concatenate([mall[t * sides + i] for i in range(sides)], axis=0)
        full[...] += jnp.dot(act[t], rows, preferred_element_type=F32)
        return carry

    full[...] = jnp.zeros_like(full)
    lax.fori_loop(0, blocks, partial, 0)
    piece = width // replicas
    for d in range(replicas):
        lo = d * piece // LANES * LANES
        hi = -(-(d + 1) * piece // LANES) * LANES
        shift = d * piece - lo
        value = full[:, lo:hi]
        if shift:
            value = pltpu.roll(value, hi - lo - shift, 1)
        part[d] = value[:, :piece]
    for r in range(1, replicas):
        part_copy(r).start()
    for r in range(1, replicas):
        part_copy(r).wait()
    total = part[rep]
    for r in range(1, replicas):
        total = total + part_got[r - 1]
    wg_out[...] = total

    own.wait()
    for r in range(1, n):
        hidden_copy(r).wait()

    def sent(t, carry):
        @pl.when((a - t >= 0) & (a + 1 < line))
        def _():
            up_copy(t, mall.at[me]).wait_send()

        @pl.when((a + t < line) & (a > 0))
        def _():
            down_copy(t, mall.at[me]).wait_send()

        side_copy(t, mall.at[me]).wait_send()
        return carry

    lax.fori_loop(0, line, sent, 0)


def fused(merged_grad, merged_owner, merger_pre, fc2_weight, query, key_states, value_states, out_grad, position):
    rows_here, width = merged_grad.shape
    n, replicas = lax.axis_size("ctx"), lax.axis_size("dp")
    slots, units = merger_pre.shape
    mine = units // n
    block, blocks = 2 * rows_here, n // 2
    piece = width // replicas
    cosine, sine = rope_tables(position)
    pre = jnp.transpose(merger_pre).reshape(n, mine, slots)
    owner = jnp.broadcast_to(merged_owner.reshape(1, rows_here), (8, rows_here))
    vmem = pl.BlockSpec(memory_space=pltpu.VMEM)
    dma = pltpu.SemaphoreType.DMA
    like = jax.ShapeDtypeStruct(query.shape, BF16)
    hidden, weight, *attention = pl.pallas_call(
        functools.partial(fused_kernel, n, replicas),
        in_specs=[vmem] * 10,
        out_specs=[vmem] * 5,
        out_shape=[
            jax.ShapeDtypeStruct((n, mine, slots), BF16),
            jax.ShapeDtypeStruct((mine, piece), F32),
            like,
            like,
            like,
        ],
        scratch_shapes=[
            pltpu.VMEM((n, rows_here, width), BF16),
            pltpu.VMEM((n, 8, rows_here), jnp.int32),
            pltpu.VMEM((n, mine, slots), BF16),
            pltpu.VMEM((blocks, 8, block), F32),
            pltpu.VMEM((blocks, mine, block), BF16),
            pltpu.VMEM((blocks, mine, block), BF16),
            pltpu.VMEM((n, mine, slots), BF16),
            pltpu.VMEM((mine, width), F32),
            pltpu.VMEM((replicas, mine, piece), F32),
            pltpu.VMEM((replicas - 1, mine, piece), F32),
            dma((n,)),
            dma((blocks,)),
            dma((blocks,)),
            dma((blocks,)),
            dma((n - 1,)),
            dma((n - 1,)),
            dma((n - 1,)),
            dma((n - 1,)),
            dma((n - 1,)),
            dma((n - 1,)),
            dma((replicas - 1,)),
            dma((replicas - 1,)),
            dma((4,)),
        ],
        compiler_params=pltpu.CompilerParams(
            collective_id=0, has_side_effects=True, vmem_limit_bytes=60 * 2**20
        ),
        name="fused",
    )(merged_grad, owner, pre, fc2_weight, query, key_states, value_states, out_grad, cosine, sine)
    hidden_grad = jnp.transpose(hidden.reshape(units, slots))
    weight_grad = weight * (rows_here * n * replicas) ** (-0.5)
    return (hidden_grad, weight_grad, *attention)


def solution(mesh):
    every = P(("dp", "ctx"), None)
    return jax.shard_map(
        fused,
        mesh=mesh,
        in_specs=(every, every, every, P("ctx", None)) + (every,) * 4 + (P(None, ("dp", "ctx")),),
        out_specs=(every, P("ctx", "dp")) + (every,) * 3,
        check_vma=False,
    )
```
